32 devices in a mesh: hst: 2 (over core), row: 4 (over y, x), col: 4 (over z).
Axes of the slice: x: 2, y: 2, z: 4, core: 2. Of those that a mesh axis runs over, the one named last changes fastest.
Arguments:
- tables: bfloat16 [256, 1024, 128], P(('hst', 'row', 'col')), may hold values from -6 to 6
- indices: int32 [256, 512, 4], P(('hst', 'row', 'col')), may hold values from 0 to 1023
- lengths: int32 [256, 512], P(('hst', 'row', 'col')), may hold values from 1 to 4, as said below
- table_slot: int32 [256], replicated, may hold values from 0 to 255, each once
- dense_feature: bfloat16 [512, 128], P(('hst', 'row', 'col')), may hold values from -48 to 48
- left_proj: bfloat16 [128, 257], replicated, may hold values from -0.375 to 0.375
- right_proj: bfloat16 [128, 257], replicated, may hold values from -0.375 to 0.375
Outputs:
- interaction: bfloat16 [512, 16384], P(('hst', 'row', 'col'))
The draws below stay inside these ranges and needn't reach their ends.
Inputs may be any that keep to these rules, and one draw needn't show every extreme that they name: Each bag uses its first lengths ids; some bag holds 4 ids.
All inputs are finite; a program needn't handle non-finite values.
Results may differ from the reference program's by a relative error of at most 0.0063.
Values may be sent and summed in bfloat16 or wider, within the bound.
No kernel may reach another device: no remote copies, remote signals or barrier semaphores. Data moves between devices by JAX's collectives and lax.ppermute only.
A program may use at most 64 MiB of HBM per device.

```python
import jax
import jax.numpy as jnp
from jax import lax

E = 128
K = 128
ROWS = 1024
BAG = 4
B_DEV = 16
TABLES = 256
BATCH = 512


def draw_lengths(key, part):
    keys_all = jax.random.split(jax.random.fold_in(key, 7), 3)
    ceiling = jax.random.randint(keys_all[0], (TABLES,), 1, BAG + 1)
    chosen = jax.random.randint(keys_all[1], (), 0, TABLES)
    table_ids = jnp.arange(TABLES, dtype=jnp.int32)
    ceiling = jnp.where(table_ids == chosen, BAG, ceiling)
    random_bits = jax.random.randint(keys_all[2], (TABLES, BATCH), 0, 1 << 20)
    result = 1 + random_bits % ceiling[:, None]
    sample_ids = jnp.arange(BATCH, dtype=jnp.int32)
    forced = (table_ids[:, None] == chosen) & (sample_ids[None, :] == 0)
    return jnp.where(forced, BAG, result).astype(jnp.int32)


def with_ends(values, rng, low, top_value):
    spot = [jax.random.randint(jax.random.fold_in(rng, axis), (), 0, length) for axis, length in enumerate(values.shape)]
    main_axis = values.shape.index(max(values.shape))
    beside = spot[:main_axis] + [(spot[main_axis] + 1) % values.shape[main_axis]] + spot[main_axis + 1:]
    return values.at[tuple(spot)].set(low).at[tuple(beside)].set(top_value)


def shard_levels(stream_key, shape, shards, low, top_value):
    level = 1.0
    for dim, shards_of in shards:
        draws = jax.random.uniform(jax.random.fold_in(jax.random.fold_in(stream_key, 6), dim), (shards_of,), jnp.float32, low / len(shards), top_value / len(shards))
        level = level * jnp.repeat(jnp.exp(draws), shape[dim] // shards_of).reshape((-1,) + (1,) * (len(shape) - 1 - dim))
    return level


def centred(rng, shape, scale, bound, cuts=(), kind=jnp.bfloat16):
    values = scale * jax.random.normal(rng, shape, jnp.float32)
    if cuts:
        values = values * shard_levels(rng, shape, cuts, -0.22, 0.18)
    return jnp.clip(values, -bound, bound).astype(kind)


def setup_inputs(seed: int = 0) -> dict:
    streams_of = jax.random.split(jax.random.key(seed), 8)
    tables = centred(streams_of[0], (TABLES, ROWS, E), 1.0, 6.0, ((0, 32),))
    indices = with_ends(jax.random.randint(streams_of[1], (TABLES, BATCH, BAG), 0, ROWS), jax.random.fold_in(streams_of[1], 1), 0, ROWS - 1).astype(jnp.int32)
    lengths = draw_lengths(jax.random.fold_in(streams_of[7], 71), 0)
    table_slot = jax.random.permutation(streams_of[3], TABLES).astype(jnp.int32)
    dense_feature = centred(streams_of[4], (BATCH, E), 8.0, 48.0, ((0, 32),))
    left_proj = centred(streams_of[5], (K, TABLES + 1), (TABLES + 1) ** -0.5, 0.375)
    right_proj = centred(streams_of[6], (K, TABLES + 1), (TABLES + 1) ** -0.5, 0.375)
    return dict(tables=tables, indices=indices, lengths=lengths, table_slot=table_slot, dense_feature=dense_feature, left_proj=left_proj, right_proj=right_proj)


def reference(tables, indices, lengths, table_slot, dense_feature, left_proj, right_proj):
    table_ids = jnp.arange(TABLES, dtype=jnp.int32)[:, None]

    def one_block(start):
        row_ids = lax.dynamic_slice_in_dim(indices, start, B_DEV, 1)
        bag_lens = lax.dynamic_slice_in_dim(lengths, start, B_DEV, 1)
        dense_rows = lax.dynamic_slice_in_dim(dense_feature, start, B_DEV, 0)
        summed = jnp.zeros((TABLES, B_DEV, E), jnp.float32)
        for position in range(BAG):
            fetched = tables[table_ids, row_ids[:, :, position]].astype(jnp.float32)
            summed = summed + jnp.where((position < bag_lens)[:, :, None], fetched, 0.0)
        pooled = summed.astype(jnp.bfloat16)
        features = jnp.concatenate([dense_rows[None], pooled[table_slot]], axis=0).astype(jnp.float32)
        left_side = jnp.einsum("kg,gbe->kbe", left_proj.astype(jnp.float32), features).astype(jnp.bfloat16)
        right_side = jnp.einsum("kg,gbe->kbe", right_proj.astype(jnp.float32), features).astype(jnp.bfloat16)
        products = jnp.einsum("kbe,lbe->bkl", left_side.astype(jnp.float32), right_side.astype(jnp.float32))
        return (products * (1.0 / E)).reshape(B_DEV, K * K).astype(jnp.bfloat16)

    starts = jnp.arange(BATCH // B_DEV, dtype=jnp.int32) * B_DEV
    return lax.map(one_block, starts).reshape(BATCH, K * K)
```

```python
import jax
import jax.numpy as jnp
from jax import lax
from jax.experimental import pallas as pl
from jax.experimental.pallas import tpu as pltpu
from jax.sharding import PartitionSpec as P

AXES = ("hst", "row", "col")
ROW_BLOCK = 256
SAMPLE_BLOCK = 512


def pool_kernel(ids_ref, lens_ref, table_ref, out_ref):
    table = pl.program_id(0)
    bag_size, samples = ids_ref.shape[1], ids_ref.shape[2]
    rows = table_ref.shape[1]
    one = jnp.ones((), jnp.bfloat16)
    zero = jnp.zeros((), jnp.bfloat16)
    ids = ids_ref[0]
    used = lax.broadcasted_iota(jnp.int32, ids.shape, 0) < lens_ref[pl.ds(table, 1), :]
    ids = jnp.where(used, ids, -1)
    row_iota = lax.broadcasted_iota(jnp.int32, (ROW_BLOCK, samples), 0).astype(jnp.float32).astype(jnp.bfloat16)
    total = None
    for start in range(0, rows, ROW_BLOCK):
        here = (ids - start).astype(jnp.float32).astype(jnp.bfloat16)
        counts = None
        for position in range(bag_size):
            hit = jnp.where(here[position : position + 1, :] == row_iota, one, zero)
            counts = hit if counts is None else counts + hit
        part = lax.dot_general(
            table_ref[0, start : start + ROW_BLOCK, :],
            counts,
            (((0,), (0,)), ((), ())),
            preferred_element_type=jnp.float32,
        )
        total = part if total is None else total + part
    out_ref[...] = total.T.astype(jnp.bfloat16).reshape(out_ref.shape)


def pool(tables, ids, lens, devices):
    tab_dev, rows, width = tables.shape
    bag_size, samples = ids.shape[1], ids.shape[2]
    own = samples // devices
    block = min(SAMPLE_BLOCK, samples)
    return pl.pallas_call(
        pool_kernel,
        grid=(tab_dev, samples // block),
        in_specs=[
            pl.BlockSpec((1, bag_size, block), lambda t, s: (t, 0, s)),
            pl.BlockSpec((tab_dev, block), lambda t, s: (0, s)),
            pl.BlockSpec((1, rows, width), lambda t, s: (t, 0, 0)),
        ],
        out_specs=pl.BlockSpec((block // own, 1, own, width), lambda t, s: (s, t, 0, 0)),
        out_shape=jax.ShapeDtypeStruct((devices, tab_dev, own, width), jnp.bfloat16),
        cost_estimate=pl.CostEstimate(
            flops=2 * tab_dev * rows * samples * width,
            bytes_accessed=2 * (tables.size + tab_dev * samples * width),
            transcendentals=0,
        ),
        name="pool",
    )(ids, lens, tables)


def shards(tables, indices, lengths, table_slot, dense_feature, left_proj, right_proj):
    tab_dev, all_samples, bag_size = indices.shape
    feature_width = tables.shape[2]
    devices = lax.axis_size(AXES)
    own_samples = all_samples // devices
    proj_rows = left_proj.shape[0]
    tables_total = left_proj.shape[1] - 1
    blocks = pool(tables, indices.transpose(0, 2, 1), lengths, devices)
    positions = jnp.arange(tables_total, dtype=jnp.int32)
    projections = jnp.concatenate([left_proj, right_proj], axis=0)
    selector = (table_slot[:, None] == positions[None, :]).astype(jnp.bfloat16)
    proj_here = jnp.dot(projections[:, 1:], selector, preferred_element_type=jnp.float32).astype(jnp.bfloat16)
    received = lax.all_to_all(blocks, AXES, split_axis=0, concat_axis=0, tiled=True)
    flattened = received.reshape(tables_total, own_samples * feature_width)
    mixed_all = jnp.dot(proj_here, flattened, preferred_element_type=jnp.float32)
    mixed_all = mixed_all.reshape(2 * proj_rows, own_samples, feature_width)
    dense_column = projections[:, 0].astype(jnp.float32)
    mixed_all = mixed_all + dense_column[:, None, None] * dense_feature[None].astype(jnp.float32)
    mixed_all = mixed_all.astype(jnp.bfloat16)
    left_side = mixed_all[:proj_rows]
    right_side = mixed_all[proj_rows:]
    products = jnp.einsum("kbe,lbe->bkl", left_side, right_side, preferred_element_type=jnp.float32)
    products = products * (1.0 / feature_width)
    return products.reshape(own_samples, proj_rows * proj_rows).astype(jnp.bfloat16)


def solution(mesh):
    in_specs = (
        P(AXES, None, None),
        P(AXES, None, None),
        P(AXES, None),
        P(),
        P(AXES, None),
        P(),
        P(),
    )
    out_specs = P(AXES, None)
    return jax.shard_map(shards, mesh=mesh, in_specs=in_specs, out_specs=out_specs, check_vma=False)
```

```python
import jax
import jax.numpy as jnp
from jax import lax
from jax.experimental import pallas as pl
from jax.experimental.pallas import tpu as pltpu
from jax.sharding import PartitionSpec as P

AXES = ("hst", "row", "col")
ROW_BLOCK = 256
SAMPLE_BLOCK = 256
TABLE_BLOCK = 4


def pool_kernel(ids_ref, lens_ref, table_ref, out_ref):
    tables, bag_size, samples = ids_ref.shape
    rows = table_ref.shape[1]
    own = out_ref.shape[2]
    first = pl.program_id(0) * tables
    block = min(SAMPLE_BLOCK, samples)
    zero = jnp.zeros((), jnp.bfloat16)
    row_iota = lax.broadcasted_iota(jnp.int32, (ROW_BLOCK, block), 0).astype(jnp.float32).astype(jnp.bfloat16)
    for table in range(tables):
        for at in range(0, samples, block):
            bag = ids_ref[table, :, at : at + block]
            used = lax.broadcasted_iota(jnp.int32, bag.shape, 0) < lens_ref[pl.ds(first + table, 1), at : at + block]
            bag = jnp.where(used, bag, -1)
            ids = [bag[j : j + 1] for j in range(bag_size)]
            times = [jnp.ones_like(ids[0]) for _ in range(bag_size)]
            for later in range(1, bag_size):
                for earlier in range(later):
                    same = ids[earlier] == ids[later]
                    times[earlier] = times[earlier] + jnp.where(same, times[later], 0)
                    ids[later] = jnp.where(same, -1, ids[later])
                    times[later] = jnp.where(same, 0, times[later])
            times = [t.astype(jnp.float32).astype(jnp.bfloat16) for t in times]
            total = None
            for start in range(0, rows, ROW_BLOCK):
                counts = zero
                for j in range(bag_size):
                    here = (ids[j] - start).astype(jnp.float32).astype(jnp.bfloat16)
                    counts = jnp.where(here == row_iota, times[j], counts)
                part = lax.dot_general(
                    table_ref[table, start : start + ROW_BLOCK, :],
                    counts,
                    (((0,), (0,)), ((), ())),
                    preferred_element_type=jnp.float32,
                )
                total = part if total is None else total + part
            out_ref[at // own : (at + block) // own, table] = (
                total.T.astype(jnp.bfloat16).reshape(block // own, own, total.shape[0])
            )


def pool(tables, ids, lens, devices):
    tab_dev, rows, width = tables.shape
    bag_size, samples = ids.shape[1], ids.shape[2]
    own = samples // devices
    return pl.pallas_call(
        pool_kernel,
        grid=(tab_dev // TABLE_BLOCK,),
        in_specs=[
            pl.BlockSpec((TABLE_BLOCK, bag_size, samples), lambda t: (t, 0, 0)),
            pl.BlockSpec((tab_dev, samples), lambda t: (0, 0)),
            pl.BlockSpec((TABLE_BLOCK, rows, width), lambda t: (t, 0, 0)),
        ],
        out_specs=pl.BlockSpec((devices, TABLE_BLOCK, own, width), lambda t: (0, t, 0, 0)),
        out_shape=jax.ShapeDtypeStruct((devices, tab_dev, own, width), jnp.bfloat16),
        cost_estimate=pl.CostEstimate(
            flops=2 * tab_dev * rows * samples * width,
            bytes_accessed=2 * (tables.size + tab_dev * samples * width),
            transcendentals=0,
        ),
        name="pool",
    )(ids, lens, tables)


def shards(tables, indices, lengths, table_slot, dense_feature, left_proj, right_proj):
    tab_dev, all_samples, bag_size = indices.shape
    feature_width = tables.shape[2]
    devices = lax.axis_size(AXES)
    own_samples = all_samples // devices
    proj_rows = left_proj.shape[0]
    tables_total = left_proj.shape[1] - 1
    blocks = pool(tables, indices.transpose(0, 2, 1), lengths, devices)
    positions = jnp.arange(tables_total, dtype=jnp.int32)
    projections = jnp.concatenate([left_proj, right_proj], axis=0)
    selector = (table_slot[:, None] == positions[None, :]).astype(jnp.bfloat16)
    proj_here = jnp.dot(projections[:, 1:], selector, preferred_element_type=jnp.float32).astype(jnp.bfloat16)
    received = lax.all_to_all(blocks, AXES, split_axis=0, concat_axis=0, tiled=True)
    flattened = received.reshape(tables_total, own_samples * feature_width)
    mixed_all = jnp.dot(proj_here, flattened, preferred_element_type=jnp.float32)
    mixed_all = mixed_all.reshape(2 * proj_rows, own_samples, feature_width)
    dense_column = projections[:, 0].astype(jnp.float32)
    mixed_all = mixed_all + dense_column[:, None, None] * dense_feature[None].astype(jnp.float32)
    mixed_all = mixed_all.astype(jnp.bfloat16)
    left_side = mixed_all[:proj_rows]
    right_side = mixed_all[proj_rows:]
    products = jnp.einsum("kbe,lbe->bkl", left_side, right_side, preferred_element_type=jnp.float32)
    products = products * (1.0 / feature_width)
    return products.reshape(own_samples, proj_rows * proj_rows).astype(jnp.bfloat16)


def solution(mesh):
    in_specs = (
        P(AXES, None, None),
        P(AXES, None, None),
        P(AXES, None),
        P(),
        P(AXES, None),
        P(),
        P(),
    )
    out_specs = P(AXES, None)
    return jax.shard_map(shards, mesh=mesh, in_specs=in_specs, out_specs=out_specs, check_vma=False)
```

```python
import functools

import jax
import jax.numpy as jnp
from jax import lax
from jax.experimental import pallas as pl
from jax.experimental.pallas import tpu as pltpu
from jax.sharding import PartitionSpec as P

AXES = ("hst", "row", "col")
PLANE = ("hst", "row")
LINE = "col"
ROW_BLOCK = 256
SAMPLE_BLOCK = 256
VMEM_LIMIT = 24 * 1024 * 1024
EARLY = 3
TABLE_BLOCK = 4


def pool_table(ids_ref, lens_ref, table_ref, table, slot, write):
    bag_size, samples = ids_ref.shape[1:]
    rows = table_ref.shape[1]
    block = min(SAMPLE_BLOCK, samples)
    zero = jnp.zeros((), jnp.bfloat16)
    row_iota = lax.broadcasted_iota(jnp.int32, (ROW_BLOCK, block), 0).astype(jnp.float32).astype(jnp.bfloat16)
    for at in range(0, samples, block):
        bag = ids_ref[slot, :, at : at + block]
        used = lax.broadcasted_iota(jnp.int32, bag.shape, 0) < lens_ref[pl.ds(table, 1), at : at + block]
        bag = jnp.where(used, bag, -1)
        ids = [bag[j : j + 1] for j in range(bag_size)]
        times = [jnp.ones_like(ids[0]) for _ in range(bag_size)]
        for later in range(1, bag_size):
            for earlier in range(later):
                same = ids[earlier] == ids[later]
                times[earlier] = times[earlier] + jnp.where(same, times[later], 0)
                ids[later] = jnp.where(same, -1, ids[later])
                times[later] = jnp.where(same, 0, times[later])
        times = [t.astype(jnp.float32).astype(jnp.bfloat16) for t in times]
        total = None
        for start in range(0, rows, ROW_BLOCK):
            counts = zero
            for j in range(bag_size):
                here = (ids[j] - start).astype(jnp.float32).astype(jnp.bfloat16)
                counts = jnp.where(here == row_iota, times[j], counts)
            part = lax.dot_general(
                table_ref[slot, start : start + ROW_BLOCK, :],
                counts,
                (((0,), (0,)), ((), ())),
                preferred_element_type=jnp.float32,
            )
            total = part if total is None else total + part
        write(at, block, total.T.astype(jnp.bfloat16))


def pool_kernel(early, steps, ids_ref, lens_ref, table_ref, *refs):
    columns = (len(refs) - 4) // 2
    near, far = refs[:columns], refs[columns]
    near_bufs, (far_buf, held, sems) = refs[columns + 1 : 2 * columns + 1], refs[2 * columns + 1 :]
    step_tables = table_ref.shape[0]
    own, width = held.shape[1:]
    plane, column = lax.axis_index(PLANE), lax.axis_index(LINE)
    copies = [pltpu.make_async_copy(near_bufs[r], near[r], sems.at[r]) for r in range(columns)]
    for step in range(steps):

        @pl.when(pl.program_id(0) == step)
        def _(step=step):
            for slot in range(step_tables):
                table = step * step_tables + slot

                def write(at, block, pooled):
                    pooled = pooled.reshape(block // own, own, width)
                    if table < early:
                        held[at // own : (at + block) // own] = pooled
                    else:
                        far_buf[at // own : (at + block) // own, table - early] = pooled

                pool_table(ids_ref, lens_ref, table_ref, table, slot, write)
                if table < early:
                    for r in range(columns):
                        for p in range(near_bufs[r].shape[0]):
                            device = lax.bitwise_xor(plane, p) * columns + lax.bitwise_xor(column, r)
                            near_bufs[r][p, table] = held[device]
                if table == early - 1:
                    for copy in copies:
                        copy.start()
            if step == steps - 1:
                last = pltpu.make_async_copy(far_buf, far, sems.at[columns])
                last.start()
                for copy in copies:
                    copy.wait()
                last.wait()


def pool(tables, ids, lens, early, planes, columns):
    tab_dev, rows, width = tables.shape
    bag_size, samples = ids.shape[1], ids.shape[2]
    devices = planes * columns
    own = samples // devices
    steps = tab_dev // TABLE_BLOCK
    near = (planes, early, own, width)
    far = (devices, tab_dev - early, own, width)
    shapes = [near] * columns + [far]
    outs = pl.pallas_call(
        functools.partial(pool_kernel, early, steps),
        grid=(steps,),
        in_specs=[
            pl.BlockSpec((TABLE_BLOCK, bag_size, samples), lambda t: (t, 0, 0)),
            pl.BlockSpec((tab_dev, samples), lambda t: (0, 0)),
            pl.BlockSpec((TABLE_BLOCK, rows, width), lambda t: (t, 0, 0)),
        ],
        out_specs=[pl.BlockSpec(memory_space=pl.ANY)] * len(shapes),
        out_shape=[jax.ShapeDtypeStruct(shape, jnp.bfloat16) for shape in shapes],
        scratch_shapes=[pltpu.VMEM(shape, jnp.bfloat16) for shape in shapes]
        + [pltpu.VMEM((devices, own, width), jnp.bfloat16), pltpu.SemaphoreType.DMA((len(shapes),))],
        cost_estimate=pl.CostEstimate(
            flops=2 * tab_dev * rows * samples * width,
            bytes_accessed=2 * tab_dev * (rows + samples) * width,
            transcendentals=0,
        ),
        name="pool",
    )(ids, lens, tables)
    return outs[:-1], outs[-1]


def by_sample(blocks):
    own, width = blocks.shape[-2:]
    return jnp.swapaxes(blocks.reshape(-1, own, width), 0, 1)


def gather_kernel(*refs):
    out_ref = refs[-1]
    at = 0
    for ref in refs[:-1]:
        part = by_sample(ref[...])
        out_ref[:, at : at + part.shape[1]] = part
        at += part.shape[1]


def gather_early(pieces):
    own, width = pieces[0].shape[-2:]
    rows = sum(piece.size for piece in pieces) // (own * width)
    vmem = pl.BlockSpec(memory_space=pltpu.VMEM)
    return pl.pallas_call(
        gather_kernel,
        in_specs=[vmem] * len(pieces),
        out_specs=vmem,
        out_shape=jax.ShapeDtypeStruct((own, rows, width), jnp.bfloat16),
        compiler_params=pltpu.CompilerParams(vmem_limit_bytes=VMEM_LIMIT),
        name="gather_early",
    )(*pieces)


def interact_kernel(early_ref, late_ref, proj_ref, dense_proj_ref, dense_ref, out_ref):
    own, width = dense_ref.shape
    proj_rows = proj_ref.shape[0] // 2
    late = by_sample(late_ref[...])
    features = jnp.concatenate([jnp.concatenate([early_ref[b], late[b]], 0) for b in range(own)], 1)
    mixed = jnp.dot(proj_ref[...], features, preferred_element_type=jnp.float32)
    dense_proj = jnp.broadcast_to(dense_proj_ref[...].astype(jnp.float32), (8, 2 * proj_rows)).T[:, :1]
    dense = dense_ref[...].astype(jnp.float32)
    products = []
    for b in range(own):
        sides = (mixed[:, b * width : (b + 1) * width] + dense_proj * dense[b : b + 1]).astype(jnp.bfloat16)
        product = lax.dot_general(
            sides[:proj_rows], sides[proj_rows:], (((1,), (1,)), ((), ())), preferred_element_type=jnp.float32
        )
        products.append((product * (1.0 / width)).astype(jnp.bfloat16))
    by_row = jnp.swapaxes(jnp.stack(products), 0, 1)
    for row in range(proj_rows):
        out_ref[:, row * proj_rows : (row + 1) * proj_rows] = by_row[row]


def interact(early, late, proj, dense_proj, dense):
    own, _ = dense.shape
    proj_rows = proj.shape[0] // 2
    vmem = pl.BlockSpec(memory_space=pltpu.VMEM)
    return pl.pallas_call(
        interact_kernel,
        in_specs=[vmem] * 5,
        out_specs=vmem,
        out_shape=jax.ShapeDtypeStruct((own, proj_rows * proj_rows), jnp.bfloat16),
        compiler_params=pltpu.CompilerParams(vmem_limit_bytes=VMEM_LIMIT),
        name="interact",
    )(early, late, proj, dense_proj, dense)


def shards(tables, indices, lengths, table_slot, dense_feature, left_proj, right_proj):
    tab_dev, _, _ = indices.shape
    devices = lax.axis_size(AXES)
    columns = lax.axis_size(LINE)
    planes = lax.axis_size(PLANE)
    early = EARLY
    plane, column = lax.axis_index(PLANE), lax.axis_index(LINE)

    def swap(x, axis, size, distance):
        return lax.ppermute(x, axis, [(i, i ^ distance) for i in range(size)])

    near, blocks = pool(tables, indices.transpose(0, 2, 1), lengths, early, planes, columns)
    arrived = {r: swap(near[r], LINE, columns, r) for r in range(1, columns)}
    late = lax.all_to_all(blocks, AXES, split_axis=0, concat_axis=0, tiled=True)
    stacked = [jnp.stack([near[0][p]] + [arrived[r][p] for r in range(1, columns)]) for p in range(planes)]
    pieces = [stacked[0]] + [swap(stacked[p], PLANE, planes, p) for p in range(1, planes)]
    features = gather_early(pieces)
    p, r, t = jnp.meshgrid(jnp.arange(planes), jnp.arange(columns), jnp.arange(early), indexing="ij")
    early_slots = ((plane ^ p) * columns + (column ^ r)) * tab_dev + t
    d, t = jnp.meshgrid(jnp.arange(devices), jnp.arange(early, tab_dev), indexing="ij")
    slots = jnp.concatenate([early_slots.reshape(-1), (d * tab_dev + t).reshape(-1)])
    selector = (table_slot[:, None] == slots[None, :]).astype(jnp.bfloat16)
    projections = jnp.concatenate([left_proj, right_proj], axis=0)
    proj = jnp.dot(projections[:, 1:], selector, preferred_element_type=jnp.float32).astype(jnp.bfloat16)
    dense_proj = projections[:, 0][None]
    return interact(features, late, proj, dense_proj, dense_feature)


def solution(mesh):
    in_specs = (
        P(AXES, None, None),
        P(AXES, None, None),
        P(AXES, None),
        P(),
        P(AXES, None),
        P(),
        P(),
    )
    out_specs = P(AXES, None)
    return jax.shard_map(shards, mesh=mesh, in_specs=in_specs, out_specs=out_specs, check_vma=False)
```

```python
import functools

import jax
import jax.numpy as jnp
from jax import lax
from jax.experimental import pallas as pl
from jax.experimental.pallas import tpu as pltpu
from jax.sharding import PartitionSpec as P

AXES = ("hst", "row", "col")
PLANE = ("hst", "row")
LINE = "col"
ROW_BLOCK = 256
SAMPLE_BLOCK = 256
VMEM_LIMIT = 24 * 1024 * 1024
EARLY = 4


def pool_table(ids_ref, lens_ref, table_ref, table, slot, write):
    bag_size, samples = ids_ref.shape[1:]
    rows = table_ref.shape[1]
    block = min(SAMPLE_BLOCK, samples)
    zero = jnp.zeros((), jnp.bfloat16)
    row_iota = lax.broadcasted_iota(jnp.int32, (ROW_BLOCK, block), 0).astype(jnp.float32).astype(jnp.bfloat16)
    for at in range(0, samples, block):
        bag = ids_ref[table, :, at : at + block]
        used = lax.broadcasted_iota(jnp.int32, bag.shape, 0) < lens_ref[pl.ds(table, 1), at : at + block]
        bag = jnp.where(used, bag, -1)
        ids = [bag[j : j + 1] for j in range(bag_size)]
        times = [jnp.ones_like(ids[0]) for _ in range(bag_size)]
        for later in range(1, bag_size):
            for earlier in range(later):
                same = ids[earlier] == ids[later]
                times[earlier] = times[earlier] + jnp.where(same, times[later], 0)
                ids[later] = jnp.where(same, -1, ids[later])
                times[later] = jnp.where(same, 0, times[later])
        times = [t.astype(jnp.float32).astype(jnp.bfloat16) for t in times]
        total = None
        for start in range(0, rows, ROW_BLOCK):
            counts = zero
            for j in range(bag_size):
                here = (ids[j] - start).astype(jnp.float32).astype(jnp.bfloat16)
                counts = jnp.where(here == row_iota, times[j], counts)
            part = lax.dot_general(
                table_ref[slot, start : start + ROW_BLOCK, :],
                counts,
                (((0,), (0,)), ((), ())),
                preferred_element_type=jnp.float32,
            )
            total = part if total is None else total + part
        write(at, block, total.T.astype(jnp.bfloat16))


def pool_early_kernel(ids_hbm, lens_hbm, tables_hbm, *refs):
    near, (ids_ref, lens_ref, later_ref), (table_ref, held, sems) = refs[:-6], refs[-6:-3], refs[-3:]
    columns = len(near)
    early = table_ref.shape[0]
    own, width = held.shape[1:]
    plane, column = lax.axis_index(PLANE), lax.axis_index(LINE)
    small = [
        pltpu.make_async_copy(ids_hbm, ids_ref, sems.at[0]),
        pltpu.make_async_copy(lens_hbm, lens_ref, sems.at[1]),
    ]
    large = [
        pltpu.make_async_copy(tables_hbm.at[slot], table_ref.at[slot], sems.at[3 + slot]) for slot in range(early)
    ]
    later = pltpu.make_async_copy(tables_hbm.at[pl.ds(early, later_ref.shape[0])], later_ref, sems.at[2])
    for copy in small + large + [later]:
        copy.start()
    for copy in small:
        copy.wait()
    for slot in range(early):
        large[slot].wait()

        def write(at, block, pooled):
            held[at // own : (at + block) // own] = pooled.reshape(block // own, own, width)

        pool_table(ids_ref, lens_ref, table_ref, slot, slot, write)
        for r in range(columns):
            for p in range(near[r].shape[0]):
                device = lax.bitwise_xor(plane, p) * columns + lax.bitwise_xor(column, r)
                near[r][p, slot] = held[device]
    later.wait()


def pool_early(tables, ids, lens, early, planes, columns):
    tab_dev, rows, width = tables.shape
    samples = ids.shape[2]
    own = samples // (planes * columns)
    shapes = [jax.ShapeDtypeStruct((planes, early, own, width), jnp.bfloat16)] * columns
    shapes += [ids, lens, jax.ShapeDtypeStruct((tab_dev - early, rows, width), jnp.bfloat16)]
    outs = pl.pallas_call(
        pool_early_kernel,
        in_specs=[pl.BlockSpec(memory_space=pltpu.HBM)] * 3,
        out_specs=[pl.BlockSpec(memory_space=pltpu.VMEM)] * len(shapes),
        out_shape=[jax.ShapeDtypeStruct(shape.shape, shape.dtype) for shape in shapes],
        scratch_shapes=[
            pltpu.VMEM((early, rows, width), jnp.bfloat16),
            pltpu.VMEM((planes * columns, own, width), jnp.bfloat16),
            pltpu.SemaphoreType.DMA((3 + early,)),
        ],
        compiler_params=pltpu.CompilerParams(vmem_limit_bytes=VMEM_LIMIT),
        cost_estimate=pool_cost(early, samples, rows, width),
        name="pool_early",
    )(*[pltpu.with_memory_space_constraint(x, pltpu.HBM) for x in (ids, lens, tables)])
    return outs[:columns], outs[columns:]


def pool_late_kernel(early, ids_ref, lens_ref, table_ref, far, far_buf, sems):
    own = far.shape[2]
    copies = []
    for slot in range(table_ref.shape[0]):

        def write(at, block, pooled):
            far_buf[at // own : (at + block) // own, slot] = pooled.reshape(block // own, own, pooled.shape[1])

        pool_table(ids_ref, lens_ref, table_ref, early + slot, slot, write)
        copies.append(pltpu.make_async_copy(far_buf.at[:, slot], far.at[:, slot], sems.at[slot]))
        copies[-1].start()
    for copy in copies:
        copy.wait()


def pool_late(tables, ids, lens, early, devices):
    late, rows, width = tables.shape
    samples = ids.shape[2]
    far = (devices, late, samples // devices, width)
    return pl.pallas_call(
        functools.partial(pool_late_kernel, early),
        in_specs=[pl.BlockSpec(memory_space=pltpu.VMEM)] * 3,
        out_specs=pl.BlockSpec(memory_space=pl.ANY),
        out_shape=jax.ShapeDtypeStruct(far, jnp.bfloat16),
        scratch_shapes=[pltpu.VMEM(far, jnp.bfloat16), pltpu.SemaphoreType.DMA((late,))],
        compiler_params=pltpu.CompilerParams(vmem_limit_bytes=VMEM_LIMIT),
        cost_estimate=pool_cost(late, samples, rows, width),
        name="pool_late",
    )(ids, lens, tables)


def pool_cost(tables, samples, rows, width):
    return pl.CostEstimate(
        flops=2 * tables * rows * samples * width,
        bytes_accessed=2 * tables * (rows + samples) * width,
        transcendentals=0,
    )


def by_sample(blocks):
    own, width = blocks.shape[-2:]
    return jnp.swapaxes(blocks.reshape(-1, own, width), 0, 1)


def gather_kernel(*refs):
    out_ref = refs[-1]
    at = 0
    for ref in refs[:-1]:
        part = by_sample(ref[...])
        out_ref[:, at : at + part.shape[1]] = part
        at += part.shape[1]


def gather_early(pieces):
    own, width = pieces[0].shape[-2:]
    rows = sum(piece.size for piece in pieces) // (own * width)
    vmem = pl.BlockSpec(memory_space=pltpu.VMEM)
    return pl.pallas_call(
        gather_kernel,
        in_specs=[vmem] * len(pieces),
        out_specs=vmem,
        out_shape=jax.ShapeDtypeStruct((own, rows, width), jnp.bfloat16),
        compiler_params=pltpu.CompilerParams(vmem_limit_bytes=VMEM_LIMIT),
        name="gather_early",
    )(*pieces)


def interact_kernel(early_ref, late_ref, proj_ref, dense_proj_ref, dense_ref, out_ref):
    own, width = dense_ref.shape
    proj_rows = proj_ref.shape[0] // 2
    late = by_sample(late_ref[...])
    features = jnp.concatenate([jnp.concatenate([early_ref[b], late[b]], 0) for b in range(own)], 1)
    mixed = jnp.dot(proj_ref[...], features, preferred_element_type=jnp.float32)
    dense_proj = jnp.broadcast_to(dense_proj_ref[...].astype(jnp.float32), (8, 2 * proj_rows)).T[:, :1]
    dense = dense_ref[...].astype(jnp.float32)
    products = []
    for b in range(own):
        sides = (mixed[:, b * width : (b + 1) * width] + dense_proj * dense[b : b + 1]).astype(jnp.bfloat16)
        product = lax.dot_general(
            sides[:proj_rows], sides[proj_rows:], (((1,), (1,)), ((), ())), preferred_element_type=jnp.float32
        )
        products.append((product * (1.0 / width)).astype(jnp.bfloat16))
    by_row = jnp.swapaxes(jnp.stack(products), 0, 1)
    for row in range(proj_rows):
        out_ref[:, row * proj_rows : (row + 1) * proj_rows] = by_row[row]


def interact(early, late, proj, dense_proj, dense):
    own, _ = dense.shape
    proj_rows = proj.shape[0] // 2
    vmem = pl.BlockSpec(memory_space=pltpu.VMEM)
    return pl.pallas_call(
        interact_kernel,
        in_specs=[vmem] * 5,
        out_specs=vmem,
        out_shape=jax.ShapeDtypeStruct((own, proj_rows * proj_rows), jnp.bfloat16),
        compiler_params=pltpu.CompilerParams(vmem_limit_bytes=VMEM_LIMIT),
        name="interact",
    )(early, late, proj, dense_proj, dense)


def shards(tables, indices, lengths, table_slot, dense_feature, left_proj, right_proj):
    tab_dev, _, _ = indices.shape
    devices = lax.axis_size(AXES)
    columns = lax.axis_size(LINE)
    planes = lax.axis_size(PLANE)
    early = EARLY
    plane, column = lax.axis_index(PLANE), lax.axis_index(LINE)

    def swap(x, axis, size, distance):
        return lax.ppermute(x, axis, [(i, i ^ distance) for i in range(size)])

    near, (ids, lens, later) = pool_early(tables, indices.transpose(0, 2, 1), lengths, early, planes, columns)
    arrived = {r: swap(near[r], LINE, columns, r) for r in range(1, columns)}
    blocks = pool_late(later, ids, lens, early, devices)
    late = lax.all_to_all(blocks, AXES, split_axis=0, concat_axis=0, tiled=True)
    stacked = [jnp.stack([near[0][p]] + [arrived[r][p] for r in range(1, columns)]) for p in range(planes)]
    pieces = [stacked[0]] + [swap(stacked[p], PLANE, planes, p) for p in range(1, planes)]
    features = gather_early(pieces)
    p, r, t = jnp.meshgrid(jnp.arange(planes), jnp.arange(columns), jnp.arange(early), indexing="ij")
    early_slots = ((plane ^ p) * columns + (column ^ r)) * tab_dev + t
    d, t = jnp.meshgrid(jnp.arange(devices), jnp.arange(early, tab_dev), indexing="ij")
    slots = jnp.concatenate([early_slots.reshape(-1), (d * tab_dev + t).reshape(-1)])
    selector = (table_slot[:, None] == slots[None, :]).astype(jnp.bfloat16)
    projections = jnp.concatenate([left_proj, right_proj], axis=0)
    proj = jnp.dot(projections[:, 1:], selector, preferred_element_type=jnp.float32).astype(jnp.bfloat16)
    dense_proj = projections[:, 0][None]
    return interact(features, late, proj, dense_proj, dense_feature)


def solution(mesh):
    in_specs = (
        P(AXES, None, None),
        P(AXES, None, None),
        P(AXES, None),
        P(),
        P(AXES, None),
        P(),
        P(),
    )
    out_specs = P(AXES, None)
    return jax.shard_map(shards, mesh=mesh, in_specs=in_specs, out_specs=out_specs, check_vma=False)
```

```python
import functools

import jax
import jax.numpy as jnp
from jax import lax
from jax.experimental import pallas as pl
from jax.experimental.pallas import tpu as pltpu
from jax.sharding import PartitionSpec as P


AXES = ("hst", "row", "col")
PLANE = ("hst", "row")
LINE = "col"
ROW_BLOCK = 256
GROUP = 64
SAMPLE_BLOCK = 256
VMEM_LIMIT = 24 * 1024 * 1024
EARLY = 4
AHEAD = 1


def count_ids(ids_ref, lens_ref, table, at, block, rows):
    bag_size = ids_ref.shape[1]
    bag = ids_ref[table, :, at : at + block]
    used = lax.broadcasted_iota(jnp.int32, bag.shape, 0) < lens_ref[pl.ds(table, 1), at : at + block]
    low = lax.bitwise_and(bag, GROUP - 1).astype(jnp.int16)
    group = jnp.where(used, lax.shift_right_logical(bag, GROUP.bit_length() - 1), -1).astype(jnp.int16)
    row_iota = lax.broadcasted_iota(jnp.int32, (GROUP, block), 0).astype(jnp.int16)
    one, zero = jnp.ones((), jnp.bfloat16), jnp.zeros((), jnp.bfloat16)
    hits = [jnp.where(low[j : j + 1] == row_iota, one, zero) for j in range(bag_size)]
    groups = [jnp.broadcast_to(group[j : j + 1], (GROUP, block)) for j in range(bag_size)]
    for later in range(1, bag_size):
        for earlier in range(later):
            same = groups[earlier] == groups[later]
            hits[earlier] = hits[earlier] + jnp.where(same, hits[later], zero)
            groups[later] = jnp.where(same, jnp.int16(-1), groups[later])
    counts = []
    for start in range(0, rows, ROW_BLOCK):
        parts = []
        for g in range(start // GROUP, (start + ROW_BLOCK) // GROUP):
            total = zero
            for j in range(bag_size):
                total = jnp.where(groups[j] == jnp.int16(g), hits[j], total)
            parts.append(total)
        counts.append(jnp.concatenate(parts, 0))
    return counts


def pool_block(table_ref, slot, counts):
    total = None
    for block, count in enumerate(counts):
        part = lax.dot_general(
            table_ref[slot, block * ROW_BLOCK : (block + 1) * ROW_BLOCK, :],
            count,
            (((0,), (0,)), ((), ())),
            preferred_element_type=jnp.float32,
        )
        total = part if total is None else total + part
    return total.T.astype(jnp.bfloat16)


def sample_blocks(samples):
    block = min(SAMPLE_BLOCK, samples)
    return block, range(0, samples, block)


def pool_early_kernel(ids_hbm, lens_hbm, tables_hbm, *refs):
    near, (ids_ref, lens_ref, later_ref), (table_ref, held, sems) = refs[:-6], refs[-6:-3], refs[-3:]
    columns = len(near)
    early = table_ref.shape[0]
    own, width = held.shape[2:]
    plane, column = lax.axis_index(PLANE), lax.axis_index(LINE)
    small = [
        pltpu.make_async_copy(ids_hbm, ids_ref, sems.at[0]),
        pltpu.make_async_copy(lens_hbm, lens_ref, sems.at[1]),
    ]
    large = [
        pltpu.make_async_copy(tables_hbm.at[slot], table_ref.at[slot], sems.at[3 + slot]) for slot in range(early)
    ]
    later = pltpu.make_async_copy(tables_hbm.at[pl.ds(early, later_ref.shape[0])], later_ref, sems.at[2])
    for copy in small + large + [later]:
        copy.start()
    for copy in small:
        copy.wait()
    block, starts = sample_blocks(ids_ref.shape[2])
    rows = table_ref.shape[1]
    ahead = [count_ids(ids_ref, lens_ref, 0, at, block, rows) for at in starts[:AHEAD]]
    for slot in range(early):
        large[slot].wait()
        for n, at in enumerate(starts):
            counts = ahead[n] if slot == 0 and n < AHEAD else count_ids(ids_ref, lens_ref, slot, at, block, rows)
            pooled = pool_block(table_ref, slot, counts)
            held[at // own : (at + block) // own, slot] = pooled.reshape(block // own, own, width)
    for r in range(columns):
        for p in range(near[r].shape[0]):
            near[r][p] = held[lax.bitwise_xor(plane, p) * columns + lax.bitwise_xor(column, r)]
    later.wait()


def pool_early(tables, ids, lens, early, planes, columns):
    tab_dev, rows, width = tables.shape
    samples = ids.shape[2]
    own = samples // (planes * columns)
    shapes = [jax.ShapeDtypeStruct((planes, early, own, width), jnp.bfloat16)] * columns
    shapes += [ids, lens, jax.ShapeDtypeStruct((tab_dev - early, rows, width), jnp.bfloat16)]
    outs = pl.pallas_call(
        pool_early_kernel,
        in_specs=[pl.BlockSpec(memory_space=pltpu.HBM)] * 3,
        out_specs=[pl.BlockSpec(memory_space=pltpu.VMEM)] * len(shapes),
        out_shape=[jax.ShapeDtypeStruct(shape.shape, shape.dtype) for shape in shapes],
        scratch_shapes=[
            pltpu.VMEM((early, rows, width), jnp.bfloat16),
            pltpu.VMEM((planes * columns, early, own, width), jnp.bfloat16),
            pltpu.SemaphoreType.DMA((3 + early,)),
        ],
        compiler_params=pltpu.CompilerParams(vmem_limit_bytes=VMEM_LIMIT),
        cost_estimate=pool_cost(early, samples, rows, width),
        name="pool_early",
    )(*[pltpu.with_memory_space_constraint(x, pltpu.HBM) for x in (ids, lens, tables)])
    return outs[:columns], outs[columns:]


def pool_late_kernel(early, ids_ref, lens_ref, table_ref, far, far_buf, sems):
    own = far.shape[2]
    copies = []
    block, starts = sample_blocks(ids_ref.shape[2])
    for slot in range(table_ref.shape[0]):
        for at in starts:
            counts = count_ids(ids_ref, lens_ref, early + slot, at, block, table_ref.shape[1])
            pooled = pool_block(table_ref, slot, counts)
            far_buf[at // own : (at + block) // own, slot] = pooled.reshape(block // own, own, pooled.shape[1])
        copies.append(pltpu.make_async_copy(far_buf.at[:, slot], far.at[:, slot], sems.at[slot]))
        copies[-1].start()
    for copy in copies:
        copy.wait()


def pool_late(tables, ids, lens, early, devices):
    late, rows, width = tables.shape
    samples = ids.shape[2]
    far = (devices, late, samples // devices, width)
    return pl.pallas_call(
        functools.partial(pool_late_kernel, early),
        in_specs=[pl.BlockSpec(memory_space=pltpu.VMEM)] * 3,
        out_specs=pl.BlockSpec(memory_space=pl.ANY),
        out_shape=jax.ShapeDtypeStruct(far, jnp.bfloat16),
        scratch_shapes=[pltpu.VMEM(far, jnp.bfloat16), pltpu.SemaphoreType.DMA((late,))],
        compiler_params=pltpu.CompilerParams(vmem_limit_bytes=VMEM_LIMIT),
        cost_estimate=pool_cost(late, samples, rows, width),
        name="pool_late",
    )(ids, lens, tables)


def pool_cost(tables, samples, rows, width):
    return pl.CostEstimate(
        flops=2 * tables * rows * samples * width,
        bytes_accessed=2 * tables * (rows + samples) * width,
        transcendentals=0,
    )


def by_sample(blocks):
    own, width = blocks.shape[-2:]
    return jnp.swapaxes(blocks.reshape(-1, own, width), 0, 1)


def gather_kernel(*refs):
    out_ref = refs[-1]
    at = 0
    for ref in refs[:-1]:
        part = by_sample(ref[...])
        out_ref[:, at : at + part.shape[1]] = part
        at += part.shape[1]


def gather_early(pieces):
    own, width = pieces[0].shape[-2:]
    rows = sum(piece.size for piece in pieces) // (own * width)
    vmem = pl.BlockSpec(memory_space=pltpu.VMEM)
    return pl.pallas_call(
        gather_kernel,
        in_specs=[vmem] * len(pieces),
        out_specs=vmem,
        out_shape=jax.ShapeDtypeStruct((own, rows, width), jnp.bfloat16),
        compiler_params=pltpu.CompilerParams(vmem_limit_bytes=VMEM_LIMIT),
        name="gather_early",
    )(*pieces)


def interact_kernel(early_ref, late_ref, proj_ref, dense_proj_ref, dense_ref, out_ref):
    own, width = dense_ref.shape
    proj_rows = proj_ref.shape[0] // 2
    late = by_sample(late_ref[...])
    features = jnp.concatenate([jnp.concatenate([early_ref[b], late[b]], 0) for b in range(own)], 1)
    mixed = jnp.dot(proj_ref[...], features, preferred_element_type=jnp.float32)
    dense_proj = jnp.broadcast_to(dense_proj_ref[...].astype(jnp.float32), (8, 2 * proj_rows)).T[:, :1]
    dense = dense_ref[...].astype(jnp.float32)
    products = []
    for b in range(own):
        sides = (mixed[:, b * width : (b + 1) * width] + dense_proj * dense[b : b + 1]).astype(jnp.bfloat16)
        product = lax.dot_general(
            sides[:proj_rows], sides[proj_rows:], (((1,), (1,)), ((), ())), preferred_element_type=jnp.float32
        )
        products.append((product * (1.0 / width)).astype(jnp.bfloat16))
    by_row = jnp.swapaxes(jnp.stack(products), 0, 1)
    for row in range(proj_rows):
        out_ref[:, row * proj_rows : (row + 1) * proj_rows] = by_row[row]


def interact(early, late, proj, dense_proj, dense):
    own, _ = dense.shape
    proj_rows = proj.shape[0] // 2
    vmem = pl.BlockSpec(memory_space=pltpu.VMEM)
    return pl.pallas_call(
        interact_kernel,
        in_specs=[vmem] * 5,
        out_specs=vmem,
        out_shape=jax.ShapeDtypeStruct((own, proj_rows * proj_rows), jnp.bfloat16),
        compiler_params=pltpu.CompilerParams(vmem_limit_bytes=VMEM_LIMIT),
        name="interact",
    )(early, late, proj, dense_proj, dense)


def shards(tables, indices, lengths, table_slot, dense_feature, left_proj, right_proj):
    tab_dev, _, _ = indices.shape
    devices = lax.axis_size(AXES)
    columns = lax.axis_size(LINE)
    planes = lax.axis_size(PLANE)
    early = EARLY
    plane, column = lax.axis_index(PLANE), lax.axis_index(LINE)

    def swap(x, axis, size, distance):
        return lax.ppermute(x, axis, [(i, i ^ distance) for i in range(size)])

    near, (ids, lens, later) = pool_early(tables, indices.transpose(0, 2, 1), lengths, early, planes, columns)
    arrived = {}
    for r in range(1, columns):
        arrived[r] = swap(near[r], LINE, columns, r)
    blocks = pool_late(later, ids, lens, early, devices)
    late = lax.all_to_all(blocks, AXES, split_axis=0, concat_axis=0, tiled=True)
    stacked = [jnp.stack([near[0][p]] + [arrived[r][p] for r in range(1, columns)]) for p in range(planes)]
    pieces = [stacked[0]] + [swap(stacked[p], PLANE, planes, p) for p in range(1, planes)]
    features = gather_early(pieces)
    p, r, t = jnp.meshgrid(jnp.arange(planes), jnp.arange(columns), jnp.arange(early), indexing="ij")
    early_slots = ((plane ^ p) * columns + (column ^ r)) * tab_dev + t
    d, t = jnp.meshgrid(jnp.arange(devices), jnp.arange(early, tab_dev), indexing="ij")
    slots = jnp.concatenate([early_slots.reshape(-1), (d * tab_dev + t).reshape(-1)])
    selector = (table_slot[:, None] == slots[None, :]).astype(jnp.bfloat16)
    projections = jnp.concatenate([left_proj, right_proj], axis=0)
    proj = jnp.dot(projections[:, 1:], selector, preferred_element_type=jnp.float32).astype(jnp.bfloat16)
    dense_proj = projections[:, 0][None]
    return interact(features, late, proj, dense_proj, dense_feature)


def solution(mesh):
    in_specs = (
        P(AXES, None, None),
        P(AXES, None, None),
        P(AXES, None),
        P(),
        P(AXES, None),
        P(),
        P(),
    )
    out_specs = P(AXES, None)
    return jax.shard_map(shards, mesh=mesh, in_specs=in_specs, out_specs=out_specs, check_vma=False)
```

```python
import functools

import jax
import jax.numpy as jnp
from jax import lax
from jax.experimental import pallas as pl
from jax.experimental.pallas import tpu as pltpu
from jax.sharding import PartitionSpec as P


AXES = ("hst", "row", "col")
PLANE = ("hst", "row")
LINE = "col"
ROW_BLOCK = 256
GROUP = 64
SAMPLE_BLOCK = 256
VMEM_LIMIT = 24 * 1024 * 1024
EARLY = 4
AHEAD = 2


def count_ids(ids_ref, lens_ref, table, at, block, rows):
    bag_size = ids_ref.shape[1]
    bag = ids_ref[table, :, at : at + block]
    used = lax.broadcasted_iota(jnp.int32, bag.shape, 0) < lens_ref[pl.ds(table, 1), at : at + block]
    low = lax.bitwise_and(bag, GROUP - 1).astype(jnp.int16)
    group = jnp.where(used, lax.shift_right_logical(bag, GROUP.bit_length() - 1), -1).astype(jnp.int16)
    row_iota = lax.broadcasted_iota(jnp.int32, (GROUP, block), 0).astype(jnp.int16)
    one, zero = jnp.ones((), jnp.bfloat16), jnp.zeros((), jnp.bfloat16)
    hits = [jnp.where(low[j : j + 1] == row_iota, one, zero) for j in range(bag_size)]
    groups = [jnp.broadcast_to(group[j : j + 1], (GROUP, block)) for j in range(bag_size)]
    for later in range(1, bag_size):
        for earlier in range(later):
            same = groups[earlier] == groups[later]
            hits[earlier] = hits[earlier] + jnp.where(same, hits[later], zero)
            groups[later] = jnp.where(same, jnp.int16(-1), groups[later])
    counts = []
    for start in range(0, rows, ROW_BLOCK):
        parts = []
        for g in range(start // GROUP, (start + ROW_BLOCK) // GROUP):
            total = zero
            for j in range(bag_size):
                total = jnp.where(groups[j] == jnp.int16(g), hits[j], total)
            parts.append(total)
        counts.append(jnp.concatenate(parts, 0))
    return counts


def pool_block(table_ref, slot, counts):
    total = None
    for block, count in enumerate(counts):
        part = lax.dot_general(
            table_ref[slot, block * ROW_BLOCK : (block + 1) * ROW_BLOCK, :],
            count,
            (((0,), (0,)), ((), ())),
            preferred_element_type=jnp.float32,
        )
        total = part if total is None else total + part
    return total.T.astype(jnp.bfloat16)


def sample_blocks(samples):
    block = min(SAMPLE_BLOCK, samples)
    return block, range(0, samples, block)


def pool_early_kernel(ids_hbm, lens_hbm, tables_hbm, *refs):
    near, (ids_ref, lens_ref, later_ref), (table_ref, held, sems) = refs[:-6], refs[-6:-3], refs[-3:]
    columns = len(near)
    early = table_ref.shape[0]
    own, width = held.shape[2:]
    plane, column = lax.axis_index(PLANE), lax.axis_index(LINE)
    small = [
        pltpu.make_async_copy(ids_hbm, ids_ref, sems.at[0]),
        pltpu.make_async_copy(lens_hbm, lens_ref, sems.at[1]),
    ]
    large = [
        pltpu.make_async_copy(tables_hbm.at[slot], table_ref.at[slot], sems.at[3 + slot]) for slot in range(early)
    ]
    later = pltpu.make_async_copy(tables_hbm.at[pl.ds(early, later_ref.shape[0])], later_ref, sems.at[2])
    for copy in small + large + [later]:
        copy.start()
    for copy in small:
        copy.wait()
    block, starts = sample_blocks(ids_ref.shape[2])
    rows = table_ref.shape[1]
    ahead = [count_ids(ids_ref, lens_ref, 0, at, block, rows) for at in starts[:AHEAD]]
    for copy in large:
        copy.wait()
    for slot in range(early):
        for n, at in enumerate(starts):
            counts = ahead[n] if slot == 0 and n < AHEAD else count_ids(ids_ref, lens_ref, slot, at, block, rows)
            pooled = pool_block(table_ref, slot, counts)
            held[at // own : (at + block) // own, slot] = pooled.reshape(block // own, own, width)
    for r in range(columns):
        for p in range(near[r].shape[0]):
            near[r][p] = held[lax.bitwise_xor(plane, p) * columns + lax.bitwise_xor(column, r)]
    later.wait()


def pool_early(tables, ids, lens, early, planes, columns):
    tab_dev, rows, width = tables.shape
    samples = ids.shape[2]
    own = samples // (planes * columns)
    shapes = [jax.ShapeDtypeStruct((planes, early, own, width), jnp.bfloat16)] * columns
    shapes += [ids, lens, jax.ShapeDtypeStruct((tab_dev - early, rows, width), jnp.bfloat16)]
    outs = pl.pallas_call(
        pool_early_kernel,
        in_specs=[pl.BlockSpec(memory_space=pltpu.HBM)] * 3,
        out_specs=[pl.BlockSpec(memory_space=pltpu.VMEM)] * len(shapes),
        out_shape=[jax.ShapeDtypeStruct(shape.shape, shape.dtype) for shape in shapes],
        scratch_shapes=[
            pltpu.VMEM((early, rows, width), jnp.bfloat16),
            pltpu.VMEM((planes * columns, early, own, width), jnp.bfloat16),
            pltpu.SemaphoreType.DMA((3 + early,)),
        ],
        compiler_params=pltpu.CompilerParams(vmem_limit_bytes=VMEM_LIMIT),
        cost_estimate=pool_cost(early, samples, rows, width),
        name="pool_early",
    )(*[pltpu.with_memory_space_constraint(x, pltpu.HBM) for x in (ids, lens, tables)])
    return outs[:columns], outs[columns:]


def pool_late_kernel(early, ids_ref, lens_ref, table_ref, far, far_buf, sems):
    own = far.shape[2]
    copies = []
    block, starts = sample_blocks(ids_ref.shape[2])
    for slot in range(table_ref.shape[0]):
        for at in starts:
            counts = count_ids(ids_ref, lens_ref, early + slot, at, block, table_ref.shape[1])
            pooled = pool_block(table_ref, slot, counts)
            far_buf[at // own : (at + block) // own, slot] = pooled.reshape(block // own, own, pooled.shape[1])
        copies.append(pltpu.make_async_copy(far_buf.at[:, slot], far.at[:, slot], sems.at[slot]))
        copies[-1].start()
    for copy in copies:
        copy.wait()


def pool_late(tables, ids, lens, early, devices):
    late, rows, width = tables.shape
    samples = ids.shape[2]
    far = (devices, late, samples // devices, width)
    return pl.pallas_call(
        functools.partial(pool_late_kernel, early),
        in_specs=[pl.BlockSpec(memory_space=pltpu.VMEM)] * 3,
        out_specs=pl.BlockSpec(memory_space=pl.ANY),
        out_shape=jax.ShapeDtypeStruct(far, jnp.bfloat16),
        scratch_shapes=[pltpu.VMEM(far, jnp.bfloat16), pltpu.SemaphoreType.DMA((late,))],
        compiler_params=pltpu.CompilerParams(vmem_limit_bytes=VMEM_LIMIT),
        cost_estimate=pool_cost(late, samples, rows, width),
        name="pool_late",
    )(ids, lens, tables)


def pool_cost(tables, samples, rows, width):
    return pl.CostEstimate(
        flops=2 * tables * rows * samples * width,
        bytes_accessed=2 * tables * (rows + samples) * width,
        transcendentals=0,
    )


def by_sample(blocks):
    own, width = blocks.shape[-2:]
    return jnp.swapaxes(blocks.reshape(-1, own, width), 0, 1)


def gather_kernel(*refs):
    out_ref = refs[-1]
    at = 0
    for ref in refs[:-1]:
        part = by_sample(ref[...])
        out_ref[:, at : at + part.shape[1]] = part
        at += part.shape[1]


def gather_early(pieces):
    own, width = pieces[0].shape[-2:]
    rows = sum(piece.size for piece in pieces) // (own * width)
    vmem = pl.BlockSpec(memory_space=pltpu.VMEM)
    return pl.pallas_call(
        gather_kernel,
        in_specs=[vmem] * len(pieces),
        out_specs=vmem,
        out_shape=jax.ShapeDtypeStruct((own, rows, width), jnp.bfloat16),
        compiler_params=pltpu.CompilerParams(vmem_limit_bytes=VMEM_LIMIT),
        name="gather_early",
    )(*pieces)


def interact_kernel(early_ref, late_ref, proj_ref, dense_proj_ref, dense_ref, out_ref):
    own, width = dense_ref.shape
    proj_rows = proj_ref.shape[0] // 2
    late = by_sample(late_ref[...])
    features = jnp.concatenate([jnp.concatenate([early_ref[b], late[b]], 0) for b in range(own)], 1)
    mixed = jnp.dot(proj_ref[...], features, preferred_element_type=jnp.float32)
    dense_proj = jnp.broadcast_to(dense_proj_ref[...].astype(jnp.float32), (8, 2 * proj_rows)).T[:, :1]
    dense = dense_ref[...].astype(jnp.float32)
    products = []
    for b in range(own):
        sides = (mixed[:, b * width : (b + 1) * width] + dense_proj * dense[b : b + 1]).astype(jnp.bfloat16)
        product = lax.dot_general(
            sides[:proj_rows], sides[proj_rows:], (((1,), (1,)), ((), ())), preferred_element_type=jnp.float32
        )
        products.append((product * (1.0 / width)).astype(jnp.bfloat16))
    by_row = jnp.swapaxes(jnp.stack(products), 0, 1)
    for row in range(proj_rows):
        out_ref[:, row * proj_rows : (row + 1) * proj_rows] = by_row[row]


def interact(early, late, proj, dense_proj, dense):
    own, _ = dense.shape
    proj_rows = proj.shape[0] // 2
    vmem = pl.BlockSpec(memory_space=pltpu.VMEM)
    return pl.pallas_call(
        interact_kernel,
        in_specs=[vmem] * 5,
        out_specs=vmem,
        out_shape=jax.ShapeDtypeStruct((own, proj_rows * proj_rows), jnp.bfloat16),
        compiler_params=pltpu.CompilerParams(vmem_limit_bytes=VMEM_LIMIT),
        name="interact",
    )(early, late, proj, dense_proj, dense)


def shards(tables, indices, lengths, table_slot, dense_feature, left_proj, right_proj):
    tab_dev, _, _ = indices.shape
    devices = lax.axis_size(AXES)
    columns = lax.axis_size(LINE)
    planes = lax.axis_size(PLANE)
    early = EARLY
    plane, column = lax.axis_index(PLANE), lax.axis_index(LINE)

    def swap(x, axis, size, distance):
        return lax.ppermute(x, axis, [(i, i ^ distance) for i in range(size)])

    near, (ids, lens, later) = pool_early(tables, indices.transpose(0, 2, 1), lengths, early, planes, columns)
    arrived = {}
    for r in range(1, columns):
        arrived[r] = swap(near[r], LINE, columns, r)
    blocks = pool_late(later, ids, lens, early, devices)
    late = lax.all_to_all(blocks, AXES, split_axis=0, concat_axis=0, tiled=True)
    stacked = [jnp.stack([near[0][p]] + [arrived[r][p] for r in range(1, columns)]) for p in range(planes)]
    pieces = [stacked[0]] + [swap(stacked[p], PLANE, planes, p) for p in range(1, planes)]
    features = gather_early(pieces)
    p, r, t = jnp.meshgrid(jnp.arange(planes), jnp.arange(columns), jnp.arange(early), indexing="ij")
    early_slots = ((plane ^ p) * columns + (column ^ r)) * tab_dev + t
    d, t = jnp.meshgrid(jnp.arange(devices), jnp.arange(early, tab_dev), indexing="ij")
    slots = jnp.concatenate([early_slots.reshape(-1), (d * tab_dev + t).reshape(-1)])
    selector = (table_slot[:, None] == slots[None, :]).astype(jnp.bfloat16)
    projections = jnp.concatenate([left_proj, right_proj], axis=0)
    proj = jnp.dot(projections[:, 1:], selector, preferred_element_type=jnp.float32).astype(jnp.bfloat16)
    dense_proj = projections[:, 0][None]
    return interact(features, late, proj, dense_proj, dense_feature)


def solution(mesh):
    in_specs = (
        P(AXES, None, None),
        P(AXES, None, None),
        P(AXES, None),
        P(),
        P(AXES, None),
        P(),
        P(),
    )
    out_specs = P(AXES, None)
    return jax.shard_map(shards, mesh=mesh, in_specs=in_specs, out_specs=out_specs, check_vma=False)
```
